32 devices in a mesh: tensor: 4 (over y, core), dp: 8 (over z, x).
Axes of the slice: x: 2, y: 2, z: 4, core: 2. Of those that a mesh axis runs over, the one named last changes fastest.
Arguments:
- tokens: bfloat16 [8, 2560, 1536], P('dp'), may hold values from -6 to 6
- segments: int32 [8, 2560], P('dp'), may hold values from 0 to 5, never falling along the last dimension, each value on 1 to 1280 neighbouring positions
- scaling: float32 [1536], replicated, may hold values from 0.5 to 1.5
- expansion: bfloat16 [2, 1536, 3072], P(None, None, 'tensor'), may hold values from -0.15625 to 0.15625
- stepping: bfloat16 [1536, 48], P(None, 'tensor'), may hold values from -0.15625 to 0.15625
- offsets: float32 [48], P('tensor'), may hold values from -6 to -2
- damping: float32 [48], P('tensor'), may hold values from 0 to 2.8
- feedthrough: float32 [48], P('tensor'), may hold values from 0.5 to 2
- smoothing: float32 [4, 3072], P(None, 'tensor'), may hold values from -3 to 3
- baseline: float32 [3072], P('tensor'), may hold values from -3 to 3
- selection: bfloat16 [1536, 256], replicated, may hold values from -0.15625 to 0.15625
- blurring: float32 [4, 256], replicated, may hold values from -3 to 3
- leveling: float32 [256], replicated, may hold values from -3 to 3
- gating: float32 [3072], P('tensor'), may hold values from 0.5 to 1.5
- contraction: bfloat16 [3072, 1536], P('tensor'), may hold values from -0.109375 to 0.109375
- cotangent: bfloat16 [8, 2560, 1536], P('dp'), may hold values from -6 to 6
Outputs:
- mixed: bfloat16 [8, 2560, 1536], P('dp')
- tokens_gradient: bfloat16 [8, 2560, 1536], P('dp')
- scaling_gradient: float32 [1536], replicated
- expansion_gradient: float32 [2, 1536, 3072], P(None, None, 'tensor')
- stepping_gradient: float32 [1536, 48], P(None, 'tensor')
- offsets_gradient: float32 [48], P('tensor')
- damping_gradient: float32 [48], P('tensor')
- feedthrough_gradient: float32 [48], P('tensor')
- smoothing_gradient: float32 [4, 3072], P(None, 'tensor')
- baseline_gradient: float32 [3072], P('tensor')
- selection_gradient: float32 [1536, 256], replicated
- blurring_gradient: float32 [4, 256], replicated
- leveling_gradient: float32 [256], replicated
- gating_gradient: float32 [3072], P('tensor')
- contraction_gradient: float32 [3072, 1536], P('tensor')
The draws below stay inside these ranges and needn't reach their ends.
Inputs may be any that keep to these rules, and one draw needn't show every extreme that they name: `segments`: within each sequence the ids never fall; each document is a run of equal ids of 1 to 1280 tokens, and one document has exactly 1280.
All inputs are finite; a program needn't handle non-finite values.
Results may differ from the reference program's by a relative error of at most 0.012.
Values may be sent and summed in bfloat16 or wider, within the bound.
No kernel may reach another device: no remote copies, remote signals or barrier semaphores. Data moves between devices by JAX's collectives and lax.ppermute only.
A program may use at most 256 MiB of HBM per device.

```python
import math
import jax
import jax.numpy as jnp
import numpy as np
from jax import lax

D = 1536
HEADS = 48
STATE = 128
CONV = 4
GROUP = 256
SEQ_LEN = 2560
INNER = 3072
SEQS = 8


def steps_of(own_key, dims, shards, smallest, top_value):
    gain, own = 1.0, jax.random.fold_in(own_key, 6)
    for position, blocks in shards:
        heights = jnp.exp(jax.random.uniform(jax.random.fold_in(own, position), (blocks,), jnp.float32, smallest / len(shards), top_value / len(shards)))
        gain = gain * jnp.repeat(heights, dims[position] // blocks).reshape([-1 if axis == position else 1 for axis in range(len(dims))])
    return gain


def profile(count, total, reach, skew):
    loads = [(1 << 20) // math.isqrt(standing ** skew) + 1 for standing in range(2, count + 1)]
    rest, given = total - reach - (count - 1), [1] * (count - 1)
    while rest > 0:
        candidates = [i for i in range(count - 1) if given[i] < reach]
        whole, budget = sum([loads[i] for i in candidates]), rest
        for i in candidates:
            more = min(reach - given[i], max(1, budget * loads[i] // whole), rest)
            given[i] = given[i] + more
            rest = rest - more
    return np.array([reach] + given)


def uneven(own_key, number_of, total, most, slope):
    if number_of == 2:
        one = jax.random.randint(own_key, (), max(1, total - most), min(most, total - 1) + 1)
        return jnp.stack([one, total - one])
    tallies = jnp.asarray(profile(number_of, total, most, slope), jnp.int32)
    couples = (number_of - 1) // 2
    giver, taker = tallies[1:1 + 2 * couples:2], tallies[2:2 + 2 * couples:2]
    slack = jnp.minimum(giver - 1, most - taker)
    shifted = jax.random.randint(jax.random.fold_in(own_key, 1), (couples,), 0, 1 << 20) % (slack + 1)
    tallies = tallies.at[1:1 + 2 * couples:2].set(giver - shifted).at[2:2 + 2 * couples:2].set(taker + shifted)
    return tallies[jax.random.permutation(jax.random.fold_in(own_key, 2), number_of)]


def bell_draw(key, dims, scale, reach, cuts=(), held_as=jnp.bfloat16):
    values = scale * jax.random.normal(key, dims, jnp.float32)
    if cuts:
        values = values * steps_of(key, dims, cuts, -0.22, 0.18)
    return jnp.clip(values, -reach, reach).astype(held_as)


def setup_inputs(seed: int = 0) -> dict:
    keys = jax.random.split(jax.random.key(seed), 17)
    return {
        "tokens": bell_draw(keys[0], (SEQS, SEQ_LEN, D), 1.0, 6.0, ((0, 8),)),
        "segments": jax.vmap(lambda own: jnp.searchsorted(jnp.cumsum(uneven(own, 6, SEQ_LEN, SEQ_LEN // 2, 2)), jnp.arange(SEQ_LEN), side="right"))(jax.random.split(keys[1], SEQS)).reshape((SEQS, SEQ_LEN)).astype(jnp.int32),
        "scaling": jnp.clip(1.0 + 0.1 * jax.random.normal(keys[2], (D,), jnp.float32), 0.5, 1.5),
        "expansion": bell_draw(keys[3], (2, D, INNER), D ** -0.5, 0.15625, ((2, 4),)),
        "stepping": bell_draw(keys[4], (D, HEADS), D ** -0.5, 0.15625, ((1, 4),)),
        "offsets": jnp.clip(-6.0 + 4.0 * jax.random.uniform(keys[5], (HEADS,), jnp.float32) ** steps_of(keys[5], (HEADS,), ((0, 4),), -0.2, 0.2), -6.0, -2.0),
        "damping": jnp.clip(2.8 * jax.random.uniform(keys[6], (HEADS,), jnp.float32) ** steps_of(keys[6], (HEADS,), ((0, 4),), -0.2, 0.2), 0.0, 2.8),
        "feedthrough": jnp.clip(0.5 + 1.5 * jax.random.uniform(keys[7], (HEADS,), jnp.float32) ** steps_of(keys[7], (HEADS,), ((0, 4),), -0.2, 0.2), 0.5, 2.0),
        "smoothing": bell_draw(keys[8], (CONV, INNER), CONV ** -0.5, 3.0, ((1, 4),), jnp.float32),
        "baseline": bell_draw(keys[9], (INNER,), 0.5, 3.0, ((0, 4),), jnp.float32),
        "selection": bell_draw(keys[10], (D, 2 * STATE), D ** -0.5, 0.15625),
        "blurring": bell_draw(keys[11], (CONV, 2 * STATE), CONV ** -0.5, 3.0, (), jnp.float32),
        "leveling": bell_draw(keys[12], (2 * STATE,), 0.5, 3.0, (), jnp.float32),
        "gating": jnp.clip(1.0 + 0.1 * jax.random.normal(keys[13], (INNER,), jnp.float32), 0.5, 1.5),
        "contraction": bell_draw(keys[14], (INNER, D), INNER ** -0.5, 0.109375, ((0, 4),)),
        "cotangent": bell_draw(keys[15], (SEQS, SEQ_LEN, D), 1.0, 6.0, ((0, 8),)),
    }


HIGH = lax.Precision.HIGHEST
EPS = 1e-05

@jax.custom_vjp
def low(v):
    return lax.optimization_barrier(v.astype(jnp.bfloat16)).astype(jnp.float32)

@jax.custom_vjp
def low_back(v):
    return v

def low_keep(v):
    return (low(v), None)

def low_pass(kept, grad):
    return (grad,)

def back_keep(v):
    return (v, None)

def back_low(kept, grad):
    return (low(grad),)
low.defvjp(low_keep, low_pass)
low_back.defvjp(back_keep, back_low)

def matmul(left, right):
    return jnp.dot(left, right, precision=HIGH, preferred_element_type=jnp.float32)

def conv_mask(values, kernel, offset_row, segment_row):
    kernel_len = kernel.shape[0]
    total = offset_row[None, :] + kernel[kernel_len - 1][None, :] * values
    for distance in range(1, kernel_len):
        moved = jnp.concatenate([jnp.zeros((distance, values.shape[1]), jnp.float32), values[:-distance]], axis=0)
        earlier = jnp.concatenate([jnp.full((distance,), -1, jnp.int32), segment_row[:-distance]], axis=0)
        valid = (earlier == segment_row).astype(jnp.float32)
        total = total + kernel[kernel_len - 1 - distance][None, :] * (moved * valid[:, None])
    return total

def group_scan(sequence_values, step_sizes, decay_rates, write_mat, read_mat, segment_row):
    length, head_count, head_size = sequence_values.shape
    block_count = length // GROUP
    blocks = (sequence_values.reshape(block_count, GROUP, head_count, head_size), step_sizes.reshape(block_count, GROUP, head_count), write_mat.reshape(block_count, GROUP, write_mat.shape[1]), read_mat.reshape(block_count, GROUP, read_mat.shape[1]), segment_row.reshape(block_count, GROUP))
    causal = jnp.arange(GROUP)[:, None] >= jnp.arange(GROUP)[None, :]

    def advance(carried, current):
        memory, previous = carried
        block_values, block_steps, block_write, block_read, block_labels = current
        log_decay = block_steps * decay_rates[None, :]
        cumulative = jnp.cumsum(log_decay, axis=0)
        inside = jnp.logical_and(causal, block_labels[:, None] == block_labels[None, :])[:, :, None]
        exponents = jnp.where(inside, cumulative[:, None, :] - cumulative[None, :, :], 0.0)
        decays = jnp.where(inside, jnp.exp(exponents), 0.0)
        intersections = jnp.dot(block_read, block_write.T, precision=HIGH)
        mixing = intersections[:, :, None] * decays * block_steps[None, :, :]
        result = jnp.einsum('tsh,shp->thp', mixing, block_values, precision=HIGH)
        carried_in = jnp.einsum('tn,hpn->thp', block_read, memory, precision=HIGH)
        keep_in = (block_labels == previous).astype(jnp.float32)
        result = result + (keep_in[:, None] * jnp.exp(cumulative))[:, :, None] * carried_in
        final_label = block_labels[GROUP - 1]
        to_final = jnp.where((block_labels == final_label)[:, None], jnp.exp(cumulative[GROUP - 1][None, :] - cumulative), 0.0) * block_steps
        persist = (final_label == previous).astype(jnp.float32) * jnp.exp(cumulative[GROUP - 1])
        memory = persist[:, None, None] * memory + jnp.einsum('sh,shp,sn->hpn', to_final, block_values, block_write, precision=HIGH)
        return ((memory, final_label), result)
    initial = (jnp.zeros((head_count, head_size, write_mat.shape[1]), jnp.float32), jnp.array(-1, jnp.int32))
    final_memory, outputs = lax.scan(jax.checkpoint(advance), initial, blocks)
    return outputs.reshape(length, head_count, head_size)

def mixer(gate_in, value_in, step_in, state_in, offsets, damping, feedthrough, smoothing, baseline, blurring, leveling, segment_row):
    head_count = offsets.shape[0]
    head_size = value_in.shape[1] // head_count
    state_size = state_in.shape[1] // 2
    conv_values = jax.nn.silu(conv_mask(value_in, smoothing, baseline, segment_row))
    conv_states = jax.nn.silu(conv_mask(state_in, blurring, leveling, segment_row))
    step_sizes = jax.nn.softplus(step_in + offsets[None, :])
    decay_rates = -jnp.exp(damping)
    per_head = conv_values.reshape(-1, head_count, head_size)
    scanned = group_scan(per_head, step_sizes, decay_rates, conv_states[:, :state_size], conv_states[:, state_size:], segment_row)
    mixed_heads = (scanned + feedthrough[None, :, None] * per_head).reshape(value_in.shape)
    return mixed_heads * jax.nn.silu(gate_in)

def layer(inputs, scaling, expansion, stepping, offsets, damping, feedthrough, smoothing, baseline, selection, blurring, leveling, gating, contraction, labels):
    inverse = lax.rsqrt(lax.optimization_barrier(jnp.mean(inputs * inputs, axis=-1, keepdims=True)) + EPS)
    normed = low(inputs * inverse * scaling[None, :])
    gate_proj = low_back(matmul(normed, expansion[0]))
    value_proj = low_back(matmul(normed, expansion[1]))
    step_raw = low_back(matmul(normed, stepping))
    state_raw = low_back(matmul(normed, selection))
    gated_out = mixer(gate_proj, value_proj, step_raw, state_raw, offsets, damping, feedthrough, smoothing, baseline, blurring, leveling, labels)
    rescale = lax.rsqrt(lax.optimization_barrier(jnp.mean(gated_out * gated_out, axis=-1, keepdims=True)) + EPS)
    projected = low_back(matmul(low(gated_out * gating[None, :]), contraction))
    return inputs + rescale * projected

def reference(tokens, segments, scaling, expansion, stepping, offsets, damping, feedthrough, smoothing, baseline, selection, blurring, leveling, gating, contraction, cotangent):
    params = tuple((parameter.astype(jnp.float32) for parameter in (scaling, expansion, stepping, offsets, damping, feedthrough, smoothing, baseline, selection, blurring, leveling, gating, contraction)))

    def per_sequence(totals, current):
        inputs, labels, upstream = current

        def forward(inputs_in, *weights):
            return layer(inputs_in, *weights, labels)
        result, pullback = jax.vjp(forward, inputs, *params)
        gradients = pullback(upstream)
        totals = tuple((total + piece for total, piece in zip(totals, gradients[1:])))
        return (totals, (result.astype(jnp.bfloat16), gradients[0].astype(jnp.bfloat16)))
    initial = tuple((jnp.zeros_like(parameter) for parameter in params))
    totals, (mixed_all, tokens_back) = lax.scan(per_sequence, initial, (tokens.astype(jnp.float32), segments, cotangent.astype(jnp.float32)))
    return (mixed_all, tokens_back, totals[0], totals[1], totals[2], totals[3], totals[4], totals[5], totals[6], totals[7], totals[8], totals[9], totals[10], totals[11], totals[12])
```

```python
import functools

import jax
import jax.numpy as jnp
from jax import lax
from jax.experimental import pallas as pl
from jax.experimental.pallas import tpu as pltpu
from jax.sharding import PartitionSpec as P

GROUP = 256
HEAD = 64
LANES = 128
EPS = 1e-05
LOG2E = 1.4426950408889634
MASKED = -1e30
F32 = jnp.float32
BF16 = jnp.bfloat16

NN = (((1,), (0,)), ((), ()))
NT = (((1,), (1,)), ((), ()))
TN = (((0,), (0,)), ((), ()))


def dot(left, right, dims=NN):
    return lax.dot_general(left, right, dims, preferred_element_type=F32)


def halves(value):
    high = value.astype(BF16)
    low = (value - high.astype(F32)).astype(BF16)
    return high, low


def thirds(value):
    high, rest = value.astype(BF16), None
    rest = value - high.astype(F32)
    middle = rest.astype(BF16)
    low = (rest - middle.astype(F32)).astype(BF16)
    return high, middle, low


def iota(shape, axis):
    return lax.broadcasted_iota(jnp.int32, shape, axis)


def spread_matrix(channels):
    rows = iota((2 * LANES, channels), 0) % LANES
    return (rows == iota((2 * LANES, channels), 1) // HEAD).astype(BF16)


def column(row):
    return jnp.transpose(jnp.broadcast_to(row, (LANES, row.shape[1])))


def sigmoid(value):
    return 1.0 / (1.0 + jnp.exp(-value))


def softplus(value):
    return jnp.maximum(value, 0.0) + jnp.log1p(jnp.exp(-jnp.abs(value)))


def conv_taps(ext_ref, cols, valid):
    return [ext_ref[8 - k : 8 - k + GROUP, cols] * valid[k - 1] for k in (1, 2, 3)]


def conv(current, taps, weight_ref, bias_ref, cols):
    total = bias_ref[0:1, cols] + weight_ref[3:4, cols] * current
    for k in (1, 2, 3):
        total = total + weight_ref[3 - k : 4 - k, cols] * taps[k - 1]
    return total


def lane_tiles(width):
    return [slice(j * LANES, (j + 1) * LANES) for j in range(width // LANES)]


def forward_kernel(
    tokens_ref,
    cot_ref,
    seg_ref,
    scaling_ref,
    expansion_ref,
    selection_ref,
    stepping_ref,
    contraction_ref,
    heads_ref,
    smooth_ref,
    base_ref,
    blur_ref,
    level_ref,
    gating_ref,
    normed_ref,
    gate_ref,
    value_ref,
    state_ref,
    step_ref,
    cum_ref,
    y_ref,
    back_ref,
    memory_ref,
    weighted_ref,
    partial_ref,
    stats_ref,
    meta_ref,
    value_ext,
    state_ext,
    seg_ext,
    memory,
    bias,
    cross,
    spread,
    back,
    zproj,
):
    channels = value_ref.shape[1]
    first = pl.program_id(0) == 0

    @pl.when(first)
    def _():
        value_ext[0:8, :] = jnp.zeros((8, channels), F32)
        state_ext[0:8, :] = jnp.zeros((8, 2 * LANES), F32)
        seg_ext[0:8, :] = jnp.full((8, LANES), -1.0, F32)
        memory[...] = jnp.zeros_like(memory)

    @pl.when(jnp.logical_not(first))
    def _():
        value_ext[0:8, :] = value_ext[GROUP : GROUP + 8, :]
        state_ext[0:8, :] = state_ext[GROUP : GROUP + 8, :]
        seg_ext[0:8, :] = seg_ext[GROUP : GROUP + 8, :]

    inputs = tokens_ref[...].astype(F32)
    inverse = lax.rsqrt(jnp.mean(inputs * inputs, axis=-1, keepdims=True) + EPS)
    normed = (inputs * inverse * scaling_ref[...]).astype(BF16)
    normed_ref[...] = normed

    seg_row = seg_ref[0]
    seg_col = column(seg_row)
    seg_ext[8 : 8 + GROUP, :] = seg_col
    valid = [(seg_ext[8 - k : 8 - k + GROUP, :] == seg_col).astype(F32) for k in (1, 2, 3)]
    keep = (seg_col == seg_ext[7:8, :]).astype(F32)
    last = (seg_col == seg_col[GROUP - 1 : GROUP, :]).astype(F32)
    keep_last = (seg_ext[GROUP + 7 : GROUP + 8, :] == seg_ext[7:8, :]).astype(F32)
    lane = iota((GROUP, LANES), 1)
    meta = jnp.where(lane == 0, valid[0], 0.0)
    for place, part in ((1, valid[1]), (2, valid[2]), (3, keep), (4, last), (5, seg_col)):
        meta = jnp.where(lane == place, part, meta)
    meta_ref[...] = meta
    wide = jnp.concatenate([seg_col, seg_col], axis=1)
    inside = jnp.logical_and(
        iota((GROUP, GROUP), 0) >= iota((GROUP, GROUP), 1), wide == seg_row
    )
    bias[...] = jnp.where(inside, 0.0, MASKED)

    value_ext[8 : 8 + GROUP, :] = dot(normed, expansion_ref[1])
    state_ext[8 : 8 + GROUP, :] = dot(normed, selection_ref[...])
    zproj[...] = dot(normed, expansion_ref[0])
    back[...] = dot(cot_ref[...], contraction_ref[...], NT)
    step = dot(normed, stepping_ref[...]) + heads_ref[0:1, :]
    step_ref[...] = step
    state_ref[...] = state_ext[8 : 8 + GROUP, :]
    gate_ref[...] = zproj[...].astype(BF16)
    back_ref[...] = back[...].astype(BF16)

    states = []
    for cols in lane_tiles(2 * LANES):
        current = state_ext[8 : 8 + GROUP, cols]
        pre = conv(current, conv_taps(state_ext, cols, valid), blur_ref, level_ref, cols)
        states.append((pre * sigmoid(pre)).astype(BF16))
    bmat, cmat = states
    cross[...] = dot(cmat, bmat, NT)

    dt = softplus(step)
    rates = -jnp.exp(heads_ref[1:2, :]) * LOG2E
    below = (iota((GROUP, GROUP), 0) >= iota((GROUP, GROUP), 1)).astype(BF16)
    pieces = dot(below, jnp.concatenate(thirds(dt * rates), axis=1))
    cum = pieces[:, :LANES] + pieces[:, LANES : 2 * LANES] + pieces[:, 2 * LANES :]
    cum_ref[...] = cum
    cum_rows = jnp.transpose(cum)
    final = cum[GROUP - 1 : GROUP, :]
    enter = keep * jnp.exp2(cum)
    leave = last * jnp.exp2(final - cum)
    persist = keep_last * jnp.exp2(final)
    extra = jnp.concatenate([persist, heads_ref[2:3, :], jnp.zeros((14, LANES), F32)], axis=0)
    stack = jnp.concatenate([dt, enter, leave, extra], axis=0)
    spread[...] = dot(jnp.concatenate(halves(stack), axis=1), spread_matrix(channels))

    left = iota((GROUP, LANES), 1) < HEAD
    squares = jnp.zeros((GROUP, LANES), F32)
    coupling = jnp.zeros((GROUP, LANES), F32)
    for pair, cols in enumerate(lane_tiles(channels)):
        current = value_ext[8 : 8 + GROUP, cols]
        value_ref[:, cols] = current
        pre = conv(current, conv_taps(value_ext, cols, valid), smooth_ref, base_ref, cols)
        x = pre * sigmoid(pre)
        scaled = x * spread[0:GROUP, cols]
        scaled_low = scaled.astype(BF16)
        sides = []
        for head in (2 * pair, 2 * pair + 1):
            power = cum[:, head : head + 1] - cum_rows[head : head + 1, :] + bias[...]
            mixing = (cross[...] * jnp.exp2(power)).astype(BF16)
            sides.append(dot(mixing, scaled_low))
        y = jnp.where(left, sides[0], sides[1])
        held = memory[:, cols]
        memory_ref[0, :, cols] = held
        y = y + spread[GROUP : 2 * GROUP, cols] * dot(cmat, held.astype(BF16))
        y = y + spread[3 * GROUP + 1 : 3 * GROUP + 2, cols] * x
        leaving = (scaled * spread[2 * GROUP : 3 * GROUP, cols]).astype(BF16)
        memory[:, cols] = held * spread[3 * GROUP : 3 * GROUP + 1, cols] + dot(bmat, leaving, TN)
        y_ref[:, cols] = y
        gate = zproj[:, cols]
        gated = y * (gate * sigmoid(gate))
        weighted = gated * gating_ref[0:1, cols]
        weighted_ref[:, cols] = weighted.astype(BF16)
        squares = squares + gated * gated
        coupling = coupling + weighted * back[:, cols]
    partial_ref[...] = dot(weighted_ref[...], contraction_ref[...]).astype(BF16)
    ones = jnp.ones((8, 2 * LANES), BF16)
    for place, part in ((0, squares), (1, coupling)):
        row = dot(ones, jnp.concatenate(halves(part), axis=1), NT)
        stats_ref[place : place + 1, :] = row[0:1, :]


def reverse_kernel(
    inner,
    gate_ref,
    value_ref,
    value_halo_ref,
    state_ref,
    state_halo_ref,
    step_ref,
    cum_ref,
    y_ref,
    back_ref,
    memory_ref,
    stats_ref,
    seg_ref,
    meta_ref,
    expansion_ref,
    selection_ref,
    stepping_ref,
    heads_ref,
    smooth_ref,
    base_ref,
    blur_ref,
    level_ref,
    gating_ref,
    tokens_ref,
    gate_low_ref,
    value_low_ref,
    state_low_ref,
    step_low_ref,
    total_ref,
    channel_ref,
    feature_ref,
    head_ref,
    scaling_ref,
    value_ext,
    state_ext,
    delta_ext,
    state_delta_ext,
    valid_ext,
    memory,
    bias,
    cross,
    mixed,
    spread,
    low_in,
    low_x,
    dinter,
    dcum,
    ddt,
):
    channels = value_ref.shape[1]
    first = pl.program_id(0) == 0
    final_step = pl.program_id(0) == pl.num_programs(0) - 1

    @pl.when(first)
    def _():
        delta_ext[GROUP : GROUP + 8, :] = jnp.zeros((8, channels), F32)
        state_delta_ext[GROUP : GROUP + 8, :] = jnp.zeros((8, 2 * LANES), F32)
        valid_ext[:, GROUP : GROUP + 8, :] = jnp.zeros((3, 8, LANES), F32)
        memory[...] = jnp.zeros_like(memory)
        channel_ref[...] = jnp.zeros_like(channel_ref)
        feature_ref[...] = jnp.zeros_like(feature_ref)
        head_ref[...] = jnp.zeros_like(head_ref)
        scaling_ref[...] = jnp.zeros_like(scaling_ref)

    @pl.when(jnp.logical_not(first))
    def _():
        delta_ext[GROUP : GROUP + 8, :] = delta_ext[0:8, :]
        state_delta_ext[GROUP : GROUP + 8, :] = state_delta_ext[0:8, :]
        valid_ext[:, GROUP : GROUP + 8, :] = valid_ext[:, 0:8, :]

    value_ext[0:8, :] = value_halo_ref[...]
    value_ext[8 : 8 + GROUP, :] = value_ref[...]
    state_ext[0:8, :] = state_halo_ref[...]
    state_ext[8 : 8 + GROUP, :] = state_ref[...]

    def lanes_of(place):
        return jnp.broadcast_to(meta_ref[:, place : place + 1], (GROUP, LANES))

    for k in range(3):
        valid_ext[k, 0:GROUP, :] = lanes_of(k)
    valid = [valid_ext[k, 0:GROUP, :] for k in range(3)]
    keep = lanes_of(3)
    last = lanes_of(4)
    seg_col = lanes_of(5)
    keep_last = keep[GROUP - 1 : GROUP, :]
    wide = jnp.concatenate([seg_col, seg_col], axis=1)
    inside = jnp.logical_and(
        iota((GROUP, GROUP), 0) <= iota((GROUP, GROUP), 1), wide == seg_ref[0]
    )
    bias[...] = jnp.where(inside, 0.0, MASKED)

    mean = stats_ref[0:1, :] / inner + EPS
    rescale_row = lax.rsqrt(mean)
    couple_row = rescale_row * rescale_row * rescale_row / inner * stats_ref[1:2, :]
    rescale = column(rescale_row)
    couple = column(couple_row)

    states, slopes = [], []
    for cols in lane_tiles(2 * LANES):
        current = state_ext[8 : 8 + GROUP, cols]
        pre = conv(current, conv_taps(state_ext, cols, valid), blur_ref, level_ref, cols)
        gate = sigmoid(pre)
        states.append((pre * gate).astype(BF16))
        slopes.append(gate * (1.0 + pre * (1.0 - gate)))
    bmat, cmat = states
    cross[...] = dot(bmat, cmat, NT)

    step = step_ref[...]
    dt = softplus(step)
    decay = -jnp.exp(heads_ref[1:2, :])
    cum = cum_ref[...]
    cum_rows = jnp.transpose(cum)
    final = cum[GROUP - 1 : GROUP, :]
    enter = keep * jnp.exp2(cum)
    leave = last * jnp.exp2(final - cum)
    persist = keep_last * jnp.exp2(final)
    extra = jnp.concatenate([persist, heads_ref[2:3, :], jnp.zeros((14, LANES), F32)], axis=0)
    stack = jnp.concatenate([dt, enter, leave, extra], axis=0)
    matrix = spread_matrix(channels)
    spread[...] = dot(jnp.concatenate(halves(stack), axis=1), matrix)

    left = iota((GROUP, LANES), 1) < HEAD
    mixed[...] = jnp.zeros_like(mixed)
    for pair, cols in enumerate(lane_tiles(channels)):
        current = value_ext[8 : 8 + GROUP, cols]
        taps = conv_taps(value_ext, cols, valid)
        pre = conv(current, taps, smooth_ref, base_ref, cols)
        squash = sigmoid(pre)
        x = pre * squash
        slope = squash * (1.0 + pre * (1.0 - squash))
        through = spread[3 * GROUP + 1 : 3 * GROUP + 2, cols]

        gate = gate_ref[:, cols].astype(F32)
        gate_squash = sigmoid(gate)
        gate_silu = gate * gate_squash
        y = y_ref[:, cols]
        gated = y * gate_silu
        scaled_back = rescale * back_ref[:, cols].astype(F32)
        channel_ref[0:1, cols] += jnp.sum(scaled_back * gated, axis=0, keepdims=True)
        dgated = scaled_back * gating_ref[0:1, cols] - couple * gated
        dy = dgated * gate_silu
        dgate = dgated * y * (gate_squash * (1.0 + gate * (1.0 - gate_squash)))
        gate_low_ref[:, cols] = dgate.astype(BF16)
        channel_ref[6:7, cols] += jnp.sum(dy * x, axis=0, keepdims=True)

        scaled = x * spread[0:GROUP, cols]
        scaled_low = scaled.astype(BF16)
        dy_low = dy.astype(BF16)
        low_in[:, cols] = (dy * spread[GROUP : 2 * GROUP, cols]).astype(BF16)
        leaving = spread[2 * GROUP : 3 * GROUP, cols]
        low_x[:, cols] = (scaled * leaving).astype(BF16)

        sides = []
        for side in (0, 1):
            head = 2 * pair + side
            power = cum_rows[head : head + 1, :] - cum[:, head : head + 1] + bias[...]
            decays = jnp.exp2(power)
            mixing = (cross[...] * decays).astype(BF16)
            sides.append(dot(mixing, dy_low))
            mine = left if side == 0 else jnp.logical_not(left)
            own = jnp.where(mine, scaled, 0.0).astype(BF16)
            mixed[...] += dot(own, dy_low, NT) * decays
        held = memory[:, cols]
        from_memory = leaving * dot(bmat, held.astype(BF16))
        dscaled = jnp.where(left, sides[0], sides[1]) + from_memory
        scaled_exact = scaled_low.astype(F32)
        dcum[:, cols] = dy_low.astype(F32) * (y - through * x) - scaled_exact * dscaled
        ddt[:, cols] = (dscaled * x).astype(BF16)
        tail = jnp.sum(scaled_exact * from_memory, axis=0, keepdims=True)
        kept = spread[3 * GROUP : 3 * GROUP + 1, cols]
        dinter[0:1, cols] = tail + kept * jnp.sum(
            held * memory_ref[0, :, cols], axis=0, keepdims=True
        )
        dpre = (through * dy + dscaled * spread[0:GROUP, cols]) * slope
        delta_ext[0:GROUP, cols] = dpre
        channel_ref[1:2, cols] += jnp.sum(dpre, axis=0, keepdims=True)
        channel_ref[5:6, cols] += jnp.sum(dpre * current, axis=0, keepdims=True)
        dvalue = smooth_ref[3:4, cols] * dpre
        for k in (1, 2, 3):
            channel_ref[5 - k : 6 - k, cols] += jnp.sum(
                dpre * taps[k - 1], axis=0, keepdims=True
            )
            dvalue = dvalue + smooth_ref[3 - k : 4 - k, cols] * (
                delta_ext[k : k + GROUP, cols] * valid_ext[k - 1, k : k + GROUP, :]
            )
        value_low_ref[:, cols] = dvalue.astype(BF16)

    memory_low = memory[...].astype(BF16)
    mixed_low = mixed[...].astype(BF16)
    dcmat = dot(low_in[...], memory_ref[0].astype(BF16), NT) + dot(mixed_low, bmat, TN)
    dbmat = dot(low_x[...], memory_low, NT) + dot(mixed_low, cmat)
    memory[...] = memory[...] * spread[3 * GROUP : 3 * GROUP + 1, :] + dot(
        cmat, low_in[...], TN
    )
    for place, (cols, grown) in enumerate(zip(lane_tiles(2 * LANES), (dbmat, dcmat))):
        current = state_ext[8 : 8 + GROUP, cols]
        taps = conv_taps(state_ext, cols, valid)
        dpre = grown * slopes[place]
        state_delta_ext[0:GROUP, cols] = dpre
        feature_ref[1:2, cols] += jnp.sum(dpre, axis=0, keepdims=True)
        feature_ref[5:6, cols] += jnp.sum(dpre * current, axis=0, keepdims=True)
        dstate = blur_ref[3:4, cols] * dpre
        for k in (1, 2, 3):
            feature_ref[5 - k : 6 - k, cols] += jnp.sum(
                dpre * taps[k - 1], axis=0, keepdims=True
            )
            dstate = dstate + blur_ref[3 - k : 4 - k, cols] * (
                state_delta_ext[k : k + GROUP, cols] * valid_ext[k - 1, k : k + GROUP, :]
            )
        state_low_ref[:, cols] = dstate.astype(BF16)

    high, low = halves(dcum[...])
    gather = matrix[:LANES, :]
    dcums = dot(high, gather, NT) + dot(low, gather, NT)
    ddts = dot(ddt[...], gather, NT)
    high, low = halves(dinter[...])
    tails = dot(high, gather, NT) + dot(low, gather, NT)
    above = (iota((GROUP, GROUP), 0) <= iota((GROUP, GROUP), 1)).astype(BF16)
    pieces = dot(above, jnp.concatenate(thirds(dcums), axis=1))
    dlog = pieces[:, :LANES] + pieces[:, LANES : 2 * LANES] + pieces[:, 2 * LANES :]
    dlog = dlog + tails[0:1, :]
    dstep = (dlog * decay + ddts) * sigmoid(step)
    step_low_ref[...] = dstep.astype(BF16)
    head_ref[0:1, :] += jnp.sum(dstep, axis=0, keepdims=True)
    head_ref[1:2, :] += jnp.sum(dlog * dt, axis=0, keepdims=True) * decay

    total = dot(gate_low_ref[...], expansion_ref[0], NT)
    total = total + dot(value_low_ref[...], expansion_ref[1], NT)
    total = total + dot(state_low_ref[...], selection_ref[...], NT)
    total = total + dot(step_low_ref[...], stepping_ref[...], NT)
    total_ref[...] = total.astype(BF16)
    inputs = tokens_ref[...].astype(F32)
    inverse = lax.rsqrt(jnp.mean(inputs * inputs, axis=-1, keepdims=True) + EPS)
    scaling_ref[0:1, :] += jnp.sum(total * (inputs * inverse), axis=0, keepdims=True)

    @pl.when(final_step)
    def _():
        high, low = halves(channel_ref[...])
        feeds = dot(high, gather, NT) + dot(low, gather, NT)
        head_ref[2:3, :] = feeds[6:7, :]


def whole(shape):
    return pl.BlockSpec(shape, lambda i: (0,) * len(shape), pipeline_mode=pl.Buffered(1))


def forward(tokens, cot, seg_rows, scaling, expansion, selection, stepping, contraction, heads, smooth, base, blur, level, gating):
    length, width = tokens.shape
    channels = expansion.shape[2]
    blocks = length // GROUP

    def rows(columns):
        return pl.BlockSpec((GROUP, columns), lambda i: (i, 0))

    def array(columns, dtype):
        return jax.ShapeDtypeStruct((length, columns), dtype)

    return pl.pallas_call(
        forward_kernel,
        grid=(blocks,),
        in_specs=[
            rows(width),
            rows(width),
            pl.BlockSpec((1, 1, GROUP), lambda i: (i, 0, 0)),
            whole(scaling.shape),
            whole(expansion.shape),
            whole(selection.shape),
            whole(stepping.shape),
            whole(contraction.shape),
            whole(heads.shape),
            whole(smooth.shape),
            whole(base.shape),
            whole(blur.shape),
            whole(level.shape),
            whole(gating.shape),
        ],
        out_specs=[
            rows(width),
            rows(channels),
            rows(channels),
            rows(2 * LANES),
            rows(LANES),
            rows(LANES),
            rows(channels),
            rows(channels),
            pl.BlockSpec((1, LANES, channels), lambda i: (i, 0, 0)),
            rows(channels),
            rows(width),
            pl.BlockSpec((2, GROUP), lambda i: (0, i)),
            rows(LANES),
        ],
        out_shape=[
            array(width, BF16),
            array(channels, BF16),
            array(channels, F32),
            array(2 * LANES, F32),
            array(LANES, F32),
            array(LANES, F32),
            array(channels, F32),
            array(channels, BF16),
            jax.ShapeDtypeStruct((blocks, LANES, channels), F32),
            array(channels, BF16),
            array(width, BF16),
            jax.ShapeDtypeStruct((2, length), F32),
            array(LANES, F32),
        ],
        scratch_shapes=[
            pltpu.VMEM((GROUP + 8, channels), F32),
            pltpu.VMEM((GROUP + 8, 2 * LANES), F32),
            pltpu.VMEM((GROUP + 8, LANES), F32),
            pltpu.VMEM((LANES, channels), F32),
            pltpu.VMEM((GROUP, GROUP), F32),
            pltpu.VMEM((GROUP, GROUP), F32),
            pltpu.VMEM((3 * GROUP + 16, channels), F32),
            pltpu.VMEM((GROUP, channels), F32),
            pltpu.VMEM((GROUP, channels), F32),
        ],
        compiler_params=pltpu.CompilerParams(vmem_limit_bytes=60 << 20),
        cost_estimate=pl.CostEstimate(
            flops=2 * length * width * 5 * channels, bytes_accessed=75 << 20, transcendentals=0
        ),
        name="forward",
    )(tokens, cot, seg_rows, scaling, expansion, selection, stepping, contraction, heads, smooth, base, blur, level, gating)


def reverse(inner, gate, value, state, step, cum, y, back, memory, stats, seg_rows, meta, expansion, selection, stepping, heads, smooth, base, blur, level, gating, tokens):
    length, width = tokens.shape
    channels = expansion.shape[2]
    blocks = length // GROUP

    def rows(columns):
        return pl.BlockSpec((GROUP, columns), lambda i: (blocks - 1 - i, 0))

    def halo(columns):
        return pl.BlockSpec(
            (8, columns), lambda i: (jnp.maximum((blocks - 1 - i) * (GROUP // 8) - 1, 0), 0)
        )

    def array(columns, dtype):
        return jax.ShapeDtypeStruct((length, columns), dtype)

    def kept(columns):
        return pl.BlockSpec((8, columns), lambda i: (0, 0))

    return pl.pallas_call(
        functools.partial(reverse_kernel, inner),
        grid=(blocks,),
        in_specs=[
            rows(channels),
            rows(channels),
            halo(channels),
            rows(2 * LANES),
            halo(2 * LANES),
            rows(LANES),
            rows(LANES),
            rows(channels),
            rows(channels),
            pl.BlockSpec((1, LANES, channels), lambda i: (blocks - 1 - i, 0, 0)),
            pl.BlockSpec((2, GROUP), lambda i: (0, blocks - 1 - i)),
            pl.BlockSpec((1, 1, GROUP), lambda i: (blocks - 1 - i, 0, 0)),
            rows(LANES),
            whole(expansion.shape),
            whole(selection.shape),
            whole(stepping.shape),
            whole(heads.shape),
            whole(smooth.shape),
            whole(base.shape),
            whole(blur.shape),
            whole(level.shape),
            whole(gating.shape),
            rows(width),
        ],
        out_specs=[
            rows(channels),
            rows(channels),
            rows(2 * LANES),
            rows(LANES),
            rows(width),
            kept(channels),
            kept(2 * LANES),
            kept(LANES),
            kept(width),
        ],
        out_shape=[
            array(channels, BF16),
            array(channels, BF16),
            array(2 * LANES, BF16),
            array(LANES, BF16),
            array(width, BF16),
            jax.ShapeDtypeStruct((8, channels), F32),
            jax.ShapeDtypeStruct((8, 2 * LANES), F32),
            jax.ShapeDtypeStruct((8, LANES), F32),
            jax.ShapeDtypeStruct((8, width), F32),
        ],
        scratch_shapes=[
            pltpu.VMEM((GROUP + 8, channels), F32),
            pltpu.VMEM((GROUP + 8, 2 * LANES), F32),
            pltpu.VMEM((GROUP + 8, channels), F32),
            pltpu.VMEM((GROUP + 8, 2 * LANES), F32),
            pltpu.VMEM((3, GROUP + 8, LANES), F32),
            pltpu.VMEM((LANES, channels), F32),
            pltpu.VMEM((GROUP, GROUP), F32),
            pltpu.VMEM((GROUP, GROUP), F32),
            pltpu.VMEM((GROUP, GROUP), F32),
            pltpu.VMEM((3 * GROUP + 16, channels), F32),
            pltpu.VMEM((GROUP, channels), BF16),
            pltpu.VMEM((GROUP, channels), BF16),
            pltpu.VMEM((8, channels), F32),
            pltpu.VMEM((GROUP, channels), F32),
            pltpu.VMEM((GROUP, channels), BF16),
        ],
        compiler_params=pltpu.CompilerParams(vmem_limit_bytes=60 << 20),
        cost_estimate=pl.CostEstimate(
            flops=2 * length * width * 4 * channels, bytes_accessed=75 << 20, transcendentals=0
        ),
        name="reverse",
    )(gate, value, value, state, state, step, cum, y, back, memory, stats, seg_rows, meta, expansion, selection, stepping, heads, smooth, base, blur, level, gating, tokens)


CORES = [(0, 1), (1, 0), (2, 3), (3, 2)]
CHIPS = [(0, 2), (2, 0), (1, 3), (3, 1)]


def place_of(ways, length):
    index = lax.axis_index("tensor")
    if ways == 4:
        return (index % 2) * (length // 2) + (index // 2) * (length // 4)
    return index * (length // ways)


def scatter_rows(ways, part):
    length = part.shape[0]
    if ways != 4:
        return lax.psum_scatter(part, "tensor", scatter_dimension=0, tiled=True).astype(F32)
    index = lax.axis_index("tensor")
    core, chip = index % 2, index // 2
    half, quarter = length // 2, length // 4
    sent = lax.dynamic_slice_in_dim(part, (1 - core) * half, half)
    got = lax.ppermute(sent, "tensor", CORES).astype(F32)
    away = lax.dynamic_slice_in_dim(part, core * half + (1 - chip) * quarter, quarter)
    away = away.astype(F32) + lax.dynamic_slice_in_dim(got, (1 - chip) * quarter, quarter)
    came = lax.ppermute(away.astype(BF16), "tensor", CHIPS).astype(F32)
    own = lax.dynamic_slice_in_dim(part, core * half + chip * quarter, quarter)
    own = own.astype(F32) + lax.dynamic_slice_in_dim(got, chip * quarter, quarter)
    return own + came


def gather_rows(ways, own):
    if ways != 4:
        return lax.all_gather(own, "tensor", axis=0, tiled=True)
    index = lax.axis_index("tensor")
    core, chip = index % 2, index // 2
    other = lax.ppermute(own, "tensor", CHIPS)
    pair = jnp.where(chip == 0, jnp.concatenate([own, other]), jnp.concatenate([other, own]))
    rest = lax.ppermute(pair, "tensor", CORES)
    return jnp.where(core == 0, jnp.concatenate([pair, rest]), jnp.concatenate([rest, pair]))


def per_device(
    ways,
    tokens,
    segments,
    scaling,
    expansion,
    stepping,
    offsets,
    damping,
    feedthrough,
    smoothing,
    baseline,
    selection,
    blurring,
    leveling,
    gating,
    contraction,
    cotangent,
):
    tokens, cot = tokens[0], cotangent[0]
    length, width = tokens.shape
    channels = expansion.shape[2]
    count = offsets.shape[0]
    inner = channels * ways
    seg_rows = segments[0].astype(F32).reshape(length // GROUP, 1, GROUP)
    heads = jnp.pad(jnp.stack([offsets, damping, feedthrough]), ((0, 5), (0, LANES - count)))
    steps = jnp.pad(stepping, ((0, 0), (0, LANES - count)))
    shared = (heads, smoothing, baseline[None], blurring, leveling[None], gating[None])
    (normed, gate, value, state, step, cum, y, back, memory, weighted, partial, stats, meta) = forward(
        tokens, cot, seg_rows, scaling[None], expansion, selection, steps, contraction, *shared
    )
    stats = jnp.sum(lax.all_gather(stats, "tensor"), axis=0)
    rescale = lax.rsqrt(stats[0] / inner + EPS)
    quarter = length // ways
    start = place_of(ways, length)

    summed = scatter_rows(ways, partial)
    own_tokens = lax.dynamic_slice_in_dim(tokens, start, quarter).astype(F32)
    own_rescale = lax.dynamic_slice_in_dim(rescale, start, quarter)[:, None]
    mixed = gather_rows(ways, (own_tokens + own_rescale * summed).astype(BF16))

    back_low = (rescale[:, None] * cot.astype(F32)).astype(BF16)
    contraction_part = dot(weighted, back_low, TN)
    contraction_sum = lax.psum(contraction_part.astype(BF16), "dp").astype(F32)

    (gate_low, value_low, state_low, step_low, total, channel, feature, head, scaled) = reverse(
        inner, gate, value, state, step, cum, y, back, memory, stats, seg_rows, meta, expansion, selection, steps, *shared, tokens
    )
    delta = scatter_rows(ways, total)
    own_cot = lax.dynamic_slice_in_dim(cot, start, quarter).astype(F32)
    inverse = lax.rsqrt(jnp.mean(own_tokens * own_tokens, axis=-1, keepdims=True) + EPS)
    grown = delta * scaling[None, :]
    mean = jnp.mean(grown * own_tokens, axis=-1, keepdims=True)
    through = inverse * grown - inverse * inverse * inverse * own_tokens * mean
    tokens_delta = gather_rows(ways, (own_cot + through).astype(BF16))

    gate_part = dot(normed, gate_low, TN).astype(BF16)
    value_part = dot(normed, value_low, TN).astype(BF16)
    state_part = dot(normed, state_low, TN)
    step_part = dot(normed, step_low, TN)[:, :count]
    gate_sum, value_sum = lax.psum((gate_part, value_part), "dp")
    expansion_sum = jnp.stack([gate_sum.astype(F32), value_sum.astype(F32)])
    heads_part = jnp.concatenate([head[:3, :count].reshape(-1), channel[:6].reshape(-1)])
    step_sum, small = lax.psum((step_part, heads_part), "dp")
    state_sum, scaled_sum, feature_sum = lax.psum(
        (state_part, scaled[0], feature[:6]), ("tensor", "dp")
    )
    heads_sum = small[: 3 * count].reshape(3, count)
    channel_sum = small[3 * count :].reshape(6, channels)
    return (
        mixed[None],
        tokens_delta[None],
        scaled_sum,
        expansion_sum,
        step_sum,
        heads_sum[0],
        heads_sum[1],
        heads_sum[2],
        channel_sum[2:6],
        channel_sum[1],
        state_sum,
        feature_sum[2:6],
        feature_sum[1],
        channel_sum[0],
        contraction_sum,
    )


def solution(mesh):
    return jax.shard_map(
        functools.partial(per_device, mesh.shape["tensor"]),
        mesh=mesh,
        in_specs=(
            P("dp", None, None),
            P("dp", None),
            P(),
            P(None, None, "tensor"),
            P(None, "tensor"),
            P("tensor"),
            P("tensor"),
            P("tensor"),
            P(None, "tensor"),
            P("tensor"),
            P(),
            P(),
            P(),
            P("tensor"),
            P("tensor", None),
            P("dp", None, None),
        ),
        out_specs=(
            P("dp", None, None),
            P("dp", None, None),
            P(),
            P(None, None, "tensor"),
            P(None, "tensor"),
            P("tensor"),
            P("tensor"),
            P("tensor"),
            P(None, "tensor"),
            P("tensor"),
            P(),
            P(),
            P(),
            P("tensor"),
            P("tensor", None),
        ),
        check_vma=False,
    )
```
